32 devices in a mesh: section: 8 (over z, core), ctx: 4 (over y, x).
Axes of the slice: x: 2, y: 2, z: 4, core: 2. Of those that a mesh axis runs over, the one named last changes fastest.
Arguments:
- queries: bfloat16 [8, 2, 512, 4096], P('section', None, 'ctx'), may hold values from -6 to 6
- keyvals: bfloat16 [8, 2, 2, 512, 512], P('section', None, None, 'ctx'), may hold values from -6 to 6
- saved_out: bfloat16 [8, 2, 512, 4096], P('section', None, 'ctx'), may hold values from -4 to 4
- grad_in: bfloat16 [8, 512, 4096], P('section', 'ctx'), may hold values from -6 to 6
- section_layers: int32 [8], replicated, may hold values from 1 to 2, as said below
- span_order: int32 [8], replicated, may hold values from 0 to 7, as said below
Outputs:
- grad_kv: bfloat16 [8, 2, 2, 512, 512], P('section', None, None, 'ctx')
- grad_down: bfloat16 [8, 512, 4096], P('section', 'ctx')
The draws below stay inside these ranges and needn't reach their ends.
Inputs may be any that keep to these rules, and one draw needn't show every extreme that they name: `section_layers`: some section owns 2 layers and some section owns 1. `span_order`: A permutation; entries 2 c and 2 c + 1 sum to 7.
All inputs are finite; a program needn't handle non-finite values.
Results may differ from the reference program's by a relative error of at most 0.0074.
Values may be sent and summed in bfloat16 or wider, within the bound.
No kernel may reach another device: no remote copies, remote signals or barrier semaphores. Data moves between devices by JAX's collectives and lax.ppermute only.
A program may use at most 128 MiB of HBM per device.

```python
import jax
import jax.numpy as jnp
from jax import lax

H = 32
KVH = 4
DH = 128
SLOTS = 2
SPAN = 64
SPANS = 8
TOKENS = 512
N_SECTION = 8
N_CTX = 4


def draw_queries(key, part):
    values = jnp.clip(jax.random.normal(jax.random.fold_in(key, 11), (N_SECTION, SLOTS, TOKENS, H * DH), jnp.float32), -6.0, 6.0)
    return values.astype(jnp.bfloat16)


def draw_keyvals(key, part):
    values = jnp.clip(jax.random.normal(jax.random.fold_in(key, 12), (N_SECTION, SLOTS, 2, TOKENS, KVH * DH), jnp.float32), -6.0, 6.0)
    return values.astype(jnp.bfloat16)


def draw_section_layers(key, part):
    counts = jax.random.randint(jax.random.fold_in(key, 21), (N_SECTION,), 1, SLOTS + 1)
    first = jax.random.randint(jax.random.fold_in(key, 22), (), 0, N_SECTION)
    other = (first + 1 + jax.random.randint(jax.random.fold_in(key, 23), (), 0, N_SECTION - 1)) % N_SECTION
    sections = jnp.arange(N_SECTION)
    counts = jnp.where(sections == first, 1, counts)
    counts = jnp.where(sections == other, SLOTS, counts)
    return counts.astype(jnp.int32)


def draw_span_order(key, part):
    shuffled = jax.random.permutation(jax.random.fold_in(key, 31), N_CTX)
    flipped = jax.random.randint(jax.random.fold_in(key, 32), (N_CTX,), 0, 2)
    leading = jnp.where(flipped == 1, SPANS - 1 - shuffled, shuffled)
    trailing = SPANS - 1 - leading
    return jnp.stack([leading, trailing], axis=1).reshape(SPANS).astype(jnp.int32)


def block_levels(own_key, shape, cuts, low, top_value):
    level, own = 1.0, jax.random.fold_in(own_key, 6)
    for axis_at, shards_of in cuts:
        heights = jnp.exp(jax.random.uniform(jax.random.fold_in(own, axis_at), (shards_of,), jnp.float32, low / len(cuts), top_value / len(cuts)))
        level = level * jnp.repeat(heights, shape[axis_at] // shards_of).reshape([-1 if axis == axis_at else 1 for axis in range(len(shape))])
    return level


def normal_values(stream_key, shape, scale, limit, split=(), held_as=jnp.bfloat16):
    gain = block_levels(stream_key, shape, split, -0.22, 0.18) if split else 1.0
    entries = jax.random.normal(stream_key, shape, jnp.float32) * scale * gain
    return jnp.minimum(jnp.maximum(entries, -limit), limit).astype(held_as)


def setup_inputs(seed: int = 0) -> dict:
    key_of = jax.random.split(jax.random.key(seed), 7)
    return {
        "queries": draw_queries(jax.random.fold_in(key_of[6], 71), 0),
        "keyvals": draw_keyvals(jax.random.fold_in(key_of[6], 71), 0),
        "saved_out": normal_values(key_of[2], (N_SECTION, SLOTS, TOKENS, H * DH), 0.3, 4.0, ((0, 8), (2, 4))),
        "grad_in": normal_values(key_of[3], (N_SECTION, TOKENS, H * DH), 1.0, 6.0, ((0, 8), (1, 4))),
        "section_layers": draw_section_layers(jax.random.fold_in(key_of[6], 71), 0),
        "span_order": draw_span_order(jax.random.fold_in(key_of[6], 71), 0),
    }


def layer_backward(gradient, query_flat, key_values, saved_heads, positions):
    tokens = gradient.shape[0]
    repeat = H // KVH
    score_scale = DH ** -0.5
    query_heads = query_flat.reshape(tokens, KVH, repeat, DH).astype(jnp.float32)
    grad_heads = gradient.reshape(tokens, KVH, repeat, DH).astype(jnp.float32)
    out_heads = saved_heads.reshape(tokens, KVH, repeat, DH).astype(jnp.float32)
    keys = key_values[0].reshape(tokens, KVH, DH).astype(jnp.float32)
    values = key_values[1].reshape(tokens, KVH, DH).astype(jnp.float32)
    visible = positions[None, :] <= positions[:, None]
    row_dots = jnp.sum(grad_heads * out_heads, axis=-1)

    def per_group(operands):
        query_group, grad_group, dots_group, key_group, value_group = operands
        scores = jnp.einsum('qrd,kd->rqk', query_group, key_group, precision=lax.Precision.HIGHEST) * score_scale
        scores = jnp.where(visible[None], scores, -jnp.inf)
        log_totals = jax.nn.logsumexp(scores, axis=-1)
        probs = jnp.where(visible[None], jnp.exp(scores - log_totals[..., None]), 0.0).astype(jnp.bfloat16)
        probs = lax.optimization_barrier(probs).astype(jnp.float32)
        grad_probs = jnp.einsum('qrd,kd->rqk', grad_group, value_group, precision=lax.Precision.HIGHEST)
        grad_scores = (probs * (grad_probs - dots_group.T[..., None])).astype(jnp.bfloat16)
        grad_scores = lax.optimization_barrier(grad_scores).astype(jnp.float32)
        value_grad = jnp.einsum('rqk,qrd->kd', probs, grad_group, precision=lax.Precision.HIGHEST)
        key_grad = jnp.einsum('rqk,qrd->kd', grad_scores, query_group, precision=lax.Precision.HIGHEST) * score_scale
        query_grad = jnp.einsum('rqk,kd->qrd', grad_scores, key_group, precision=lax.Precision.HIGHEST) * score_scale
        return query_grad, key_grad, value_grad

    query_grad, key_grad, value_grad = lax.map(per_group, (
        query_heads.transpose(1, 0, 2, 3), grad_heads.transpose(1, 0, 2, 3),
        row_dots.transpose(1, 0, 2), keys.transpose(1, 0, 2), values.transpose(1, 0, 2)))
    query_grad = query_grad.transpose(1, 0, 2, 3).reshape(tokens, H * DH)
    key_grad = key_grad.transpose(1, 0, 2).reshape(tokens, KVH * DH)
    value_grad = value_grad.transpose(1, 0, 2).reshape(tokens, KVH * DH)
    new_gradient = (gradient.astype(jnp.float32) + query_grad).astype(jnp.bfloat16)
    return new_gradient, jnp.stack([key_grad, value_grad]).astype(jnp.bfloat16)


def reference(queries, keyvals, saved_out, grad_in, section_layers, span_order):
    rows = jnp.arange(TOKENS, dtype=jnp.int32)
    positions = (span_order[rows // SPAN] * SPAN + rows % SPAN).astype(jnp.int32)

    def per_section(operands):
        gradient, section_queries, section_keys, section_outs, layer_count = operands
        results = [None] * SLOTS
        for slot in reversed(range(SLOTS)):
            def active(current, slot=slot):
                return layer_backward(current, section_queries[slot], section_keys[slot], section_outs[slot], positions)

            def inactive(current):
                return current, jnp.zeros((2, TOKENS, KVH * DH), jnp.bfloat16)

            gradient, key_value_grad = lax.cond(slot < layer_count, active, inactive, gradient)
            results[slot] = key_value_grad
        return jnp.stack(results), gradient

    grad_kv, finals = lax.map(per_section, (grad_in, queries, keyvals, saved_out, section_layers))
    grad_down = jnp.roll(finals, -1, axis=0)
    return grad_kv, grad_down
```

```python
import functools
import math

import jax
import jax.numpy as jnp
from jax import lax
from jax.experimental import pallas as pl
from jax.experimental.pallas import tpu as pltpu
from jax.sharding import PartitionSpec as P

DH = 128
HIDDEN = -1e30


def exchanged(array, axis, mask):
    length = lax.axis_size(axis)
    return lax.ppermute(array, axis, [(i, i ^ mask) for i in range(length)])


def shifted(array, axis, by):
    length = lax.axis_size(axis)
    return lax.ppermute(array, axis, [(i, (i + by) % length) for i in range(length)])


def layer_kernel(piece_count, targets, repeat, meta_ref, q_ref, g_ref, o_ref, *refs):
    pieces = refs[:piece_count]
    g_out_ref = refs[piece_count]
    outs = refs[piece_count + 1 : piece_count + 1 + len(targets)]
    p_s, ds_s = refs[-2:]
    tokens = q_ref.shape[0]
    span_rows = tokens // 2
    keys_total = p_s.shape[0]
    scale = DH ** (-0.5)
    pair = 2 * DH
    pair_rows = 2 * tokens

    @pl.when(meta_ref[0] == 0)
    def _():
        g_out_ref[...] = g_ref[...]
        for out in outs:
            out[...] = jnp.zeros_like(out)

    @pl.when(meta_ref[0] != 0)
    def _():
        keys = jnp.concatenate([piece[0] for piece in pieces], axis=0)
        values = jnp.concatenate([piece[1] for piece in pieces], axis=0)
        keys_t = keys.T
        lane = lax.broadcasted_iota(jnp.int32, (span_rows, tokens), 1)
        query_pos = jnp.where(
            lane < span_rows,
            meta_ref[1] * span_rows + lane,
            meta_ref[2] * span_rows + lane - span_rows,
        )
        row = lax.broadcasted_iota(jnp.int32, (span_rows, tokens), 0)
        bias = jnp.concatenate(
            [
                jnp.where(meta_ref[3 + t] * span_rows + row <= query_pos, 0.0, HIDDEN)
                for t in range(keys_total // span_rows)
            ],
            axis=0,
        )
        bias = jnp.concatenate([bias, bias], axis=1)
        ones = jnp.ones((8, 2 * DH), jnp.bfloat16)

        def heads_of(ref, index):
            return jnp.concatenate(
                [
                    ref[:, pl.ds(index * pair, DH)],
                    ref[:, pl.ds(index * pair + DH, DH)],
                ],
                axis=0,
            )

        def visit(index):
            q2 = heads_of(q_ref, index)
            g2 = heads_of(g_ref, index)
            o2 = heads_of(o_ref, index)
            product = g2.astype(jnp.float32) * o2.astype(jnp.float32)
            high = product.astype(jnp.bfloat16)
            low = (product - high.astype(jnp.float32)).astype(jnp.bfloat16)
            nt = (((1,), (1,)), ((), ()))
            row_dot = lax.dot_general(
                ones,
                jnp.concatenate([high, low], axis=1),
                nt,
                preferred_element_type=jnp.float32,
            )[0:1]
            scores = lax.dot_general(keys, q2, nt, preferred_element_type=jnp.float32)
            scores = scores + bias
            top = jnp.max(scores, axis=0, keepdims=True)
            factor = scale * math.log2(math.e)
            powers = jnp.exp2(scores * factor - top * factor)
            inverse = 1.0 / jnp.sum(powers, axis=0, keepdims=True)
            probs = (powers * inverse).astype(jnp.bfloat16)
            grad_probs = lax.dot_general(values, g2, nt, preferred_element_type=jnp.float32)
            grad_scores = (probs.astype(jnp.float32) * (grad_probs - row_dot)).astype(jnp.bfloat16)
            columns = pl.ds(index * pair_rows, pair_rows)
            p_s[:, columns] = probs
            ds_s[:, columns] = grad_scores
            query_grad = lax.dot_general(
                keys_t, grad_scores, (((1,), (0,)), ((), ())), preferred_element_type=jnp.float32
            )
            query_grad = query_grad.T * scale
            for part in range(2):
                lanes = pl.ds(index * pair + part * DH, DH)
                g_out_ref[:, lanes] = (
                    g_ref[:, lanes].astype(jnp.float32)
                    + query_grad[part * tokens : (part + 1) * tokens]
                ).astype(g_out_ref.dtype)

        if keys_total <= 512:
            for index in range(repeat // 2):
                visit(index)
        else:

            @pl.loop(0, repeat // 2)
            def _(index):
                visit(index)

        q_all = jnp.concatenate([q_ref[:, r * DH : (r + 1) * DH] for r in range(repeat)], axis=0)
        g_all = jnp.concatenate([g_ref[:, r * DH : (r + 1) * DH] for r in range(repeat)], axis=0)
        value_grad = jnp.dot(p_s[...], g_all, preferred_element_type=jnp.float32)
        key_grad = jnp.dot(ds_s[...], q_all, preferred_element_type=jnp.float32) * scale
        for out, ranges in zip(outs, targets):
            at = 0
            for start, size in ranges:
                out[0, at : at + size] = key_grad[start : start + size].astype(out.dtype)
                out[1, at : at + size] = value_grad[start : start + size].astype(out.dtype)
                at += size


def layer(meta, queries, gradient, saved_out, slot, pieces, targets, dtypes):
    tokens, width = gradient.shape
    kv_width = pieces[0].shape[-1]
    groups = kv_width // DH
    repeat = width // kv_width
    keys_total = sum(piece.shape[-2] for piece in pieces)
    head_block = pl.BlockSpec((None, None, tokens, repeat * DH), lambda e: (0, slot, 0, e))
    grad_block = pl.BlockSpec((tokens, repeat * DH), lambda e: (0, e))
    piece_specs = []
    for piece in pieces:
        if piece.ndim == 5:
            piece_specs.append(
                pl.BlockSpec((None, None, 2, piece.shape[3], DH), lambda e: (0, slot, 0, 0, e))
            )
        else:
            piece_specs.append(pl.BlockSpec((2, piece.shape[1], DH), lambda e: (0, 0, e)))
    rows = [sum(size for _, size in ranges) for ranges in targets]
    outs = pl.pallas_call(
        functools.partial(layer_kernel, len(pieces), targets, repeat),
        grid=(groups,),
        in_specs=[
            pl.BlockSpec(memory_space=pltpu.SMEM),
            head_block,
            grad_block,
            head_block,
            *piece_specs,
        ],
        out_specs=[grad_block]
        + [pl.BlockSpec((2, count, DH), lambda e: (0, 0, e)) for count in rows],
        out_shape=[jax.ShapeDtypeStruct((tokens, width), jnp.bfloat16)]
        + [
            jax.ShapeDtypeStruct((2, count, kv_width), dtype) for count, dtype in zip(rows, dtypes)
        ],
        scratch_shapes=[
            pltpu.VMEM((keys_total, repeat * tokens), jnp.bfloat16),
            pltpu.VMEM((keys_total, repeat * tokens), jnp.bfloat16),
        ],
        compiler_params=pltpu.CompilerParams(vmem_limit_bytes=48 << 20),
        cost_estimate=pl.CostEstimate(
            flops=10 * tokens * width * keys_total,
            bytes_accessed=10 * tokens * width,
            transcendentals=tokens * (width // DH) * keys_total,
        ),
        name=f"layer_{slot}",
    )(meta, queries, gradient, saved_out, *pieces)
    return outs


def on_device(queries, keyvals, saved_out, grad_in, section_layers, span_order):
    cycle = lax.axis_size("ctx")
    own = lax.axis_index("ctx")
    section = lax.axis_index("section")
    slots = queries.shape[1]
    tokens = queries.shape[2]
    half = tokens // 2
    order_rows = span_order.reshape(cycle, 2)
    layer_count = lax.dynamic_index_in_dim(section_layers, section, 0, keepdims=False)
    own_spans = lax.dynamic_index_in_dim(order_rows, own, 0, keepdims=False)
    square = cycle == 4

    if square:
        sources = jnp.stack([own, own ^ 1, own ^ 2, own ^ 3])
        key_spans = order_rows[sources].reshape(-1)
    else:
        key_spans = span_order

    def gathered(slot):
        if not square:
            return [lax.all_gather(keyvals[0, slot], "ctx", axis=1, tiled=True)]
        block = keyvals[0, slot]
        from_x = exchanged(block, "ctx", 1)
        from_y = exchanged(block, "ctx", 2)
        low = exchanged(from_y[:, :half], "ctx", 1)
        high = exchanged(from_x[:, half:], "ctx", 2)
        return [keyvals, from_x, from_y, low, high]

    if square:
        targets = (
            ((0, tokens),),
            ((3 * tokens, half), (tokens, half)),
            ((3 * tokens + half, half), (2 * tokens + half, half)),
            ((tokens + half, half),),
            ((2 * tokens, half),),
        )
        dtypes = (jnp.float32, jnp.bfloat16, jnp.bfloat16, jnp.float32, jnp.float32)
    else:
        targets = (((0, cycle * tokens),),)
        dtypes = (jnp.float32,)

    def reduced(parts):
        if not square:
            total = lax.psum_scatter(parts[0], "ctx", scatter_dimension=1, tiled=True)
            return total.astype(jnp.bfloat16)
        mine, first_x, first_y, rest_x, rest_y = parts
        got_x = exchanged(first_x, "ctx", 1)
        got_y = exchanged(first_y, "ctx", 2)
        second_x = (rest_x + got_y[:, :half].astype(jnp.float32)).astype(jnp.bfloat16)
        second_y = (rest_y + got_x[:, :half].astype(jnp.float32)).astype(jnp.bfloat16)
        more_x = exchanged(second_x, "ctx", 1)
        more_y = exchanged(second_y, "ctx", 2)
        low = (
            mine[:, :half]
            + got_x[:, half:].astype(jnp.float32)
            + more_y.astype(jnp.float32)
        )
        high = (
            mine[:, half:]
            + got_y[:, half:].astype(jnp.float32)
            + more_x.astype(jnp.float32)
        )
        return jnp.concatenate([low, high], axis=1).astype(jnp.bfloat16)

    gradient = grad_in[0]
    results = [None] * slots
    pieces = {slot: gathered(slot) for slot in reversed(range(slots))}
    for slot in reversed(range(slots)):
        live = (slot < layer_count).astype(jnp.int32)
        meta = jnp.concatenate([live[None], own_spans, key_spans]).astype(jnp.int32)
        gradient, *parts = layer(
            meta, queries, gradient, saved_out, slot, pieces[slot], targets, dtypes
        )
        results[slot] = reduced(parts)
    grad_kv = jnp.stack(results)[None]
    grad_down = shifted(gradient[None], "section", -1)
    return (grad_kv, grad_down)


def solution(mesh):
    in_specs = (
        P("section", None, "ctx", None),
        P("section", None, None, "ctx", None),
        P("section", None, "ctx", None),
        P("section", "ctx", None),
        P(),
        P(),
    )
    out_specs = (P("section", None, None, "ctx", None), P("section", "ctx", None))
    return jax.shard_map(
        on_device, mesh=mesh, in_specs=in_specs, out_specs=out_specs, check_vma=False
    )
```

```python
import functools
import math

import jax
import jax.numpy as jnp
from jax import lax
from jax.experimental import pallas as pl
from jax.experimental.pallas import tpu as pltpu
from jax.sharding import PartitionSpec as P

DH = 128
HIDDEN = -1e30
NT = (((1,), (1,)), ((), ()))


def exchanged(array, axis, mask):
    length = lax.axis_size(axis)
    return lax.ppermute(array, axis, [(i, i ^ mask) for i in range(length)])


def shifted(array, axis, by):
    length = lax.axis_size(axis)
    return lax.ppermute(array, axis, [(i, (i + by) % length) for i in range(length)])


def write_live(live, g_ref, g_out_ref, outs, compute):
    @pl.when(jnp.logical_not(live))
    def _():
        g_out_ref[...] = g_ref[...]
        for out in outs:
            out[...] = jnp.zeros_like(out)

    pl.when(live)(compute)


def row_dots(grads, outputs):
    product = grads.astype(jnp.float32) * outputs.astype(jnp.float32)
    return jnp.sum(product.T, axis=0, keepdims=True)


def softmax(scores):
    factor = DH ** (-0.5) * math.log2(math.e)
    top = jnp.max(scores, axis=0, keepdims=True)
    powers = jnp.exp2(scores * factor - top * factor)
    inverse = 1.0 / jnp.sum(powers, axis=0, keepdims=True)
    return (powers * inverse).astype(jnp.bfloat16)


def square_kernel(parts_of, targets, repeat, heads, slots, spans_ref, layers_ref, q_ref, g_ref, o_ref, *refs):
    pieces = refs[: len(parts_of)]
    g_out_ref = refs[len(parts_of)]
    outs = refs[len(parts_of) + 1 : len(parts_of) + 1 + len(targets)]
    g_s, k_s, v_s, dk_s, dv_s, p_hi, p_lo, ds_hi, ds_lo = refs[-9:]
    step = pl.program_id(0)
    live = layers_ref[lax.axis_index("section")] > slots - 1 - step
    span_rows = q_ref.shape[0] // 2
    spans = k_s.shape[1] // span_rows
    scale = DH ** (-0.5)
    own = lax.axis_index("ctx")

    @pl.when(step == 0)
    def _():
        g_s[...] = g_ref[...]

    @pl.when(step != 0)
    def _():
        g_s[...] = g_out_ref[...]

    def span_at(part):
        return spans_ref[2 * (own ^ part[0]) + part[1]]

    def rows_of(index):
        return pl.ds(pl.multiple_of(index * span_rows, span_rows), span_rows)

    def compute():
        for piece, parts in zip(pieces, parts_of):
            for at, part in enumerate(parts):
                rows = rows_of(span_at(part))
                for e in range(heads):
                    here = (slice(at * span_rows, (at + 1) * span_rows), slice(e * DH, (e + 1) * DH))
                    k_s[e, rows] = piece[(0, *here)]
                    v_s[e, rows] = piece[(1, *here)]
        first, second = spans_ref[2 * own], spans_ref[2 * own + 1]
        low_span = jnp.minimum(first, second)
        high_part = (second > first).astype(jnp.int32)

        def with_low(low):
            high = spans - 1 - low
            seen = (high + 1) * span_rows
            split = (low + 1) * span_rows
            shape = (span_rows, repeat * span_rows)
            offset = lax.rem(lax.broadcasted_iota(jnp.int32, shape, 1), span_rows)
            bias = jnp.where(lax.broadcasted_iota(jnp.int32, shape, 0) <= offset, 0.0, HIDDEN)

            def heads_of(ref, index, e):
                rows = rows_of(index)
                return jnp.concatenate(
                    [ref[rows, (e * repeat + r) * DH : (e * repeat + r + 1) * DH] for r in range(repeat)],
                    axis=0,
                )

            def chain(e, index, span, p_s, ds_s):
                rows = rows_of(index)
                size = (span + 1) * span_rows
                keys = k_s[e, :size]
                grads = heads_of(g_s, index, e)
                scores = lax.dot_general(
                    keys, heads_of(q_ref, index, e), NT, preferred_element_type=jnp.float32
                )
                last = scores[size - span_rows :] + bias
                if span:
                    last = jnp.concatenate([scores[: size - span_rows], last], axis=0)
                grad_probs = lax.dot_general(
                    v_s[e, :size], grads, NT, preferred_element_type=jnp.float32
                )
                dots = row_dots(grads, heads_of(o_ref, index, e))
                yield
                probs = softmax(last)
                grad_scores = (probs.astype(jnp.float32) * (grad_probs - dots)).astype(jnp.bfloat16)
                p_s[e, :size] = probs
                ds_s[e, :size] = grad_scores
                yield
                query_grad = jnp.dot(keys.T, grad_scores, preferred_element_type=jnp.float32)
                query_grad = query_grad.T * scale
                for r in range(repeat):
                    lanes = slice((e * repeat + r) * DH, (e * repeat + r + 1) * DH)
                    g_out_ref[rows, lanes] = (
                        g_s[rows, lanes].astype(jnp.float32)
                        + query_grad[r * span_rows : (r + 1) * span_rows]
                    ).astype(g_out_ref.dtype)
                yield

            def totals(e):
                for weights_hi, weights_lo, ref, total, factor in (
                    (p_hi, p_lo, g_s, dv_s, 1.0),
                    (ds_hi, ds_lo, q_ref, dk_s, scale),
                ):
                    right_hi = heads_of(ref, high_part, e)
                    right_lo = heads_of(ref, 1 - high_part, e)
                    near = jnp.dot(
                        jnp.concatenate([weights_hi[e, :split], weights_lo[e, :split]], axis=1),
                        jnp.concatenate([right_hi, right_lo], axis=0),
                        preferred_element_type=jnp.float32,
                    )
                    far = jnp.dot(
                        weights_hi[e, split:seen], right_hi, preferred_element_type=jnp.float32
                    )
                    total[e, :split] = near * factor
                    total[e, split:seen] = far * factor
                    if seen < total.shape[1]:
                        total[e, seen:] = jnp.zeros((total.shape[1] - seen, DH), jnp.float32)

            pending = None
            for e in range(heads):
                for one in (
                    chain(e, 1 - high_part, low, p_lo, ds_lo),
                    chain(e, high_part, high, p_hi, ds_hi),
                ):
                    next(one)
                    if pending is not None:
                        next(pending)
                        next(pending)
                    pending = one
                if e:
                    totals(e - 1)
            next(pending)
            next(pending)
            totals(heads - 1)

        for low in range(spans // 2):
            pl.when(low_span == low)(functools.partial(with_low, low))
        for out, parts in zip(outs, targets):
            for at, part in enumerate(parts):
                rows = rows_of(span_at(part))
                for e in range(heads):
                    here = (slice(at * span_rows, (at + 1) * span_rows), slice(e * DH, (e + 1) * DH))
                    out[(0, *here)] = dk_s[e, rows].astype(out.dtype)
                    out[(1, *here)] = dv_s[e, rows].astype(out.dtype)

    write_live(live, g_s, g_out_ref, outs, compute)


def general_kernel(
    slot, repeat, spans_ref, layers_ref, q_ref, g_ref, o_ref, piece, g_out_ref, out, p_s, ds_s
):
    tokens = q_ref.shape[0]
    span_rows = tokens // 2
    keys_total = p_s.shape[0]
    pair = 2 * DH
    own = lax.axis_index("ctx")

    def compute():
        keys = piece[0]
        values = piece[1]
        keys_t = keys.T
        lane = lax.broadcasted_iota(jnp.int32, (span_rows, tokens), 1)
        query_pos = jnp.where(
            lane < span_rows,
            spans_ref[2 * own] * span_rows + lane,
            (spans_ref[2 * own + 1] - 1) * span_rows + lane,
        )
        row = lax.broadcasted_iota(jnp.int32, (span_rows, tokens), 0)
        bias = jnp.concatenate(
            [
                jnp.where(spans_ref[t] * span_rows + row <= query_pos, 0.0, HIDDEN)
                for t in range(keys_total // span_rows)
            ],
            axis=0,
        )
        bias = jnp.concatenate([bias, bias], axis=1)

        @pl.loop(0, repeat // 2)
        def _(index):
            def heads_of(ref):
                return jnp.concatenate(
                    [ref[:, pl.ds(index * pair + part * DH, DH)] for part in range(2)], axis=0
                )

            grads = heads_of(g_ref)
            dots = row_dots(grads, heads_of(o_ref))
            scores = lax.dot_general(keys, heads_of(q_ref), NT, preferred_element_type=jnp.float32)
            probs = softmax(scores + bias)
            grad_probs = lax.dot_general(values, grads, NT, preferred_element_type=jnp.float32)
            grad_scores = (probs.astype(jnp.float32) * (grad_probs - dots)).astype(jnp.bfloat16)
            query_grad = jnp.dot(keys_t, grad_scores, preferred_element_type=jnp.float32)
            query_grad = query_grad.T * DH ** (-0.5)
            columns = pl.ds(index * 2 * tokens, 2 * tokens)
            p_s[:, columns] = probs
            ds_s[:, columns] = grad_scores
            for part in range(2):
                lanes = pl.ds(index * pair + part * DH, DH)
                g_out_ref[:, lanes] = (
                    g_ref[:, lanes].astype(jnp.float32)
                    + query_grad[part * tokens : (part + 1) * tokens]
                ).astype(g_out_ref.dtype)

        q_all = jnp.concatenate([q_ref[:, r * DH : (r + 1) * DH] for r in range(repeat)], axis=0)
        g_all = jnp.concatenate([g_ref[:, r * DH : (r + 1) * DH] for r in range(repeat)], axis=0)
        out[0] = jnp.dot(ds_s[...], q_all, preferred_element_type=jnp.float32) * DH ** (-0.5)
        out[1] = jnp.dot(p_s[...], g_all, preferred_element_type=jnp.float32)

    live = layers_ref[lax.axis_index("section")] > slot
    write_live(live, g_ref, g_out_ref, [out], compute)


def general_layer(slot, span_order, section_layers, queries, gradient, saved_out, piece):
    tokens, width = gradient.shape
    kv_width = piece.shape[-1]
    groups = kv_width // DH
    repeat = width // kv_width
    keys_total = piece.shape[1]
    head_block = pl.BlockSpec((None, None, tokens, repeat * DH), lambda e: (0, slot, 0, e))
    grad_block = pl.BlockSpec((tokens, repeat * DH), lambda e: (0, e))
    key_block = pl.BlockSpec((2, keys_total, DH), lambda e: (0, 0, e))
    return pl.pallas_call(
        functools.partial(general_kernel, slot, repeat),
        grid=(groups,),
        in_specs=[
            pl.BlockSpec(memory_space=pltpu.SMEM),
            pl.BlockSpec(memory_space=pltpu.SMEM),
            head_block,
            grad_block,
            head_block,
            key_block,
        ],
        out_specs=[grad_block, key_block],
        out_shape=[
            jax.ShapeDtypeStruct((tokens, width), jnp.bfloat16),
            jax.ShapeDtypeStruct((2, keys_total, kv_width), jnp.float32),
        ],
        scratch_shapes=[pltpu.VMEM((keys_total, repeat * tokens), jnp.bfloat16)] * 2,
        compiler_params=pltpu.CompilerParams(vmem_limit_bytes=48 << 20),
        name=f"layer_{slot}",
    )(span_order, section_layers, queries, gradient, saved_out, piece)


def general_device(queries, keyvals, saved_out, grad_in, section_layers, span_order):
    slots = queries.shape[1]
    gradient = grad_in[0]
    results = [None] * slots
    for slot in reversed(range(slots)):
        piece = lax.all_gather(keyvals[0, slot], "ctx", axis=1, tiled=True)
        gradient, part = general_layer(
            slot, span_order, section_layers, queries, gradient, saved_out, piece
        )
        total = lax.psum_scatter(part, "ctx", scatter_dimension=1, tiled=True)
        results[slot] = total.astype(jnp.bfloat16)
    return jnp.stack(results)[None], shifted(gradient[None], "section", -1)


PARTS = (((0, 0), (0, 1)),) + tuple(((d, p),) for d in (1, 2, 3) for p in range(2))
TARGETS = (
    ((0, 0), (0, 1)),
    ((3, 0), (1, 0)),
    ((3, 1), (2, 1)),
    ((1, 1),),
    ((2, 0),),
)
TARGET_TYPES = (jnp.float32, jnp.bfloat16, jnp.bfloat16, jnp.float32, jnp.float32)


def square_layers(start, heads, span_order, section_layers, queries, gradient, saved_out, pieces):
    slots, tokens, width = queries.shape[1:]
    repeat = width // pieces[0].shape[-1]
    half = tokens // 2
    keys_total = span_order.shape[0] * half
    lanes = heads * DH
    at = start // heads
    head_block = pl.BlockSpec(
        (None, None, tokens, repeat * lanes), lambda s: (0, slots - 1 - s, 0, at)
    )
    own_block = pl.BlockSpec(
        (None, None, 2, tokens, lanes), lambda s: (0, slots - 1 - s, 0, 0, at)
    )
    return pl.pallas_call(
        functools.partial(square_kernel, PARTS, TARGETS, repeat, heads, slots),
        grid=(slots,),
        in_specs=[
            pl.BlockSpec(memory_space=pltpu.SMEM),
            pl.BlockSpec(memory_space=pltpu.SMEM),
            head_block,
            pl.BlockSpec((None, tokens, repeat * lanes), lambda s: (0, 0, at)),
            head_block,
            own_block,
        ]
        + [pl.BlockSpec((None, 2, half, lanes), lambda s: (slots - 1 - s, 0, 0, 0))] * 6,
        out_specs=[pl.BlockSpec((tokens, repeat * lanes), lambda s: (0, 0))]
        + [
            pl.BlockSpec((None, 2, len(parts) * half, lanes), lambda s: (slots - 1 - s, 0, 0, 0))
            for parts in TARGETS
        ],
        out_shape=[jax.ShapeDtypeStruct((tokens, repeat * lanes), jnp.bfloat16)]
        + [
            jax.ShapeDtypeStruct((slots, 2, len(parts) * half, lanes), dtype)
            for parts, dtype in zip(TARGETS, TARGET_TYPES)
        ],
        scratch_shapes=[
            pltpu.VMEM((tokens, repeat * lanes), jnp.bfloat16),
            pltpu.VMEM((heads, keys_total, DH), jnp.bfloat16),
            pltpu.VMEM((heads, keys_total, DH), jnp.bfloat16),
            pltpu.VMEM((heads, keys_total, DH), jnp.float32),
            pltpu.VMEM((heads, keys_total, DH), jnp.float32),
        ]
        + [
            pltpu.VMEM((heads, rows, repeat * half), jnp.bfloat16)
            for rows in (keys_total, keys_total // 2, keys_total, keys_total // 2)
        ],
        compiler_params=pltpu.CompilerParams(vmem_limit_bytes=48 << 20),
        cost_estimate=pl.CostEstimate(
            flops=10 * slots * tokens * repeat * lanes * keys_total,
            bytes_accessed=16 * slots * tokens * repeat * lanes,
            transcendentals=slots * tokens * repeat * heads * keys_total,
        ),
        name=f"layers_{start}",
    )(span_order, section_layers, queries, gradient, saved_out, *pieces)


CHUNKS = ((0, 2), (2, 4))


def on_device(queries, keyvals, saved_out, grad_in, section_layers, span_order):
    half = queries.shape[2] // 2
    if lax.axis_size("ctx") != 4 or keyvals.shape[4] != CHUNKS[-1][1] * DH:
        return general_device(queries, keyvals, saved_out, grad_in, section_layers, span_order)

    def gathered(start, stop):
        own = keyvals[0, :, :, :, start * DH : stop * DH]
        low = own[:, :, :half]
        high = own[:, :, half:]
        x_high = exchanged(high, "ctx", 1)
        y_low = exchanged(low, "ctx", 2)
        x_low = exchanged(low, "ctx", 1)
        y_high = exchanged(high, "ctx", 2)
        far_low = exchanged(y_low, "ctx", 1)
        far_high = exchanged(x_high, "ctx", 2)
        return [keyvals, x_low, x_high, y_low, y_high, far_low, far_high]

    def reduced(mine, first_x, first_y, rest_x, rest_y):
        got_x = exchanged(first_x, "ctx", 1)
        got_y = exchanged(first_y, "ctx", 2)
        second_x = (rest_x + got_y[:, :, :half].astype(jnp.float32)).astype(jnp.bfloat16)
        second_y = (rest_y + got_x[:, :, :half].astype(jnp.float32)).astype(jnp.bfloat16)
        more_x = exchanged(second_x, "ctx", 1)
        more_y = exchanged(second_y, "ctx", 2)
        low = (
            mine[:, :, :half]
            + got_x[:, :, half:].astype(jnp.float32)
            + more_y.astype(jnp.float32)
        )
        high = (
            mine[:, :, half:]
            + got_y[:, :, half:].astype(jnp.float32)
            + more_x.astype(jnp.float32)
        )
        return jnp.concatenate([low, high], axis=2).astype(jnp.bfloat16)

    pieces = [gathered(start, stop) for start, stop in CHUNKS]
    key_parts = []
    down_parts = []
    for (start, stop), own_pieces in zip(CHUNKS, pieces):
        gradient, *parts = square_layers(
            start, stop - start, span_order, section_layers, queries, grad_in, saved_out, own_pieces
        )
        down_parts.append(shifted(gradient, "section", -1))
        key_parts.append(reduced(*parts))
    grad_kv = jnp.concatenate(key_parts, axis=3)[None]
    grad_down = jnp.concatenate(down_parts, axis=1)[None]
    return (grad_kv, grad_down)


def solution(mesh):
    in_specs = (
        P("section", None, "ctx", None),
        P("section", None, None, "ctx", None),
        P("section", None, "ctx", None),
        P("section", "ctx", None),
        P(),
        P(),
    )
    out_specs = (P("section", None, None, "ctx", None), P("section", "ctx", None))
    return jax.shard_map(
        on_device, mesh=mesh, in_specs=in_specs, out_specs=out_specs, check_vma=False
    )
```

```python
import functools
import math

import jax
import jax.numpy as jnp
from jax import lax
from jax.experimental import pallas as pl
from jax.experimental.pallas import tpu as pltpu
from jax.sharding import PartitionSpec as P

DH = 128
HIDDEN = -1e30
NT = (((1,), (1,)), ((), ()))


def exchanged(array, axis, mask):
    length = lax.axis_size(axis)
    return lax.ppermute(array, axis, [(i, i ^ mask) for i in range(length)])


def shifted(array, axis, by):
    length = lax.axis_size(axis)
    return lax.ppermute(array, axis, [(i, (i + by) % length) for i in range(length)])


def write_live(live, g_ref, g_out_ref, outs, compute):
    @pl.when(jnp.logical_not(live))
    def _():
        g_out_ref[...] = g_ref[...]
        for out in outs:
            out[...] = jnp.zeros_like(out)

    pl.when(live)(compute)


def row_dots(grads, outputs):
    product = grads.astype(jnp.float32) * outputs.astype(jnp.float32)
    return jnp.sum(product.T, axis=0, keepdims=True)


def softmax(scores):
    factor = DH ** (-0.5) * math.log2(math.e)
    top = jnp.max(scores, axis=0, keepdims=True)
    powers = jnp.exp2(scores * factor - top * factor)
    inverse = 1.0 / jnp.sum(powers, axis=0, keepdims=True)
    return (powers * inverse).astype(jnp.bfloat16)


def square_kernel(parts_of, targets, repeat, heads, slots, meta_ref, q_ref, g_ref, o_ref, *refs):
    pieces = refs[: len(parts_of)]
    g_out_ref = refs[len(parts_of)]
    outs = refs[len(parts_of) + 1 : len(parts_of) + 1 + len(targets)]
    g_s, k_s, v_s, dk_s, dv_s, p_hi, p_lo, ds_hi, ds_lo = refs[-9:]
    step = pl.program_id(0)
    live = meta_ref[k_s.shape[1] // (q_ref.shape[0] // 2) + lax.axis_index("section")] > slots - 1 - step
    span_rows = q_ref.shape[0] // 2
    spans = k_s.shape[1] // span_rows
    scale = DH ** (-0.5)
    own = lax.axis_index("ctx")

    @pl.when(step == 0)
    def _():
        g_s[...] = g_ref[...]

    @pl.when(step != 0)
    def _():
        g_s[...] = g_out_ref[...]

    def span_at(part):
        return meta_ref[2 * (own ^ part[0]) + part[1]]

    def rows_of(index):
        return pl.ds(pl.multiple_of(index * span_rows, span_rows), span_rows)

    def compute():
        for piece, parts in zip(pieces, parts_of):
            for at, part in enumerate(parts):
                rows = rows_of(span_at(part))
                for e in range(heads):
                    here = (slice(at * span_rows, (at + 1) * span_rows), slice(e * DH, (e + 1) * DH))
                    k_s[e, rows] = piece[(0, *here)]
                    v_s[e, rows] = piece[(1, *here)]
        first, second = meta_ref[2 * own], meta_ref[2 * own + 1]
        low_span = jnp.minimum(first, second)
        high_part = (second > first).astype(jnp.int32)

        def with_low(low):
            high = spans - 1 - low
            seen = (high + 1) * span_rows
            split = (low + 1) * span_rows
            shape = (span_rows, repeat * span_rows)
            offset = lax.rem(lax.broadcasted_iota(jnp.int32, shape, 1), span_rows)
            bias = jnp.where(lax.broadcasted_iota(jnp.int32, shape, 0) <= offset, 0.0, HIDDEN)

            def heads_of(ref, index, e):
                rows = rows_of(index)
                return jnp.concatenate(
                    [ref[rows, (e * repeat + r) * DH : (e * repeat + r + 1) * DH] for r in range(repeat)],
                    axis=0,
                )

            def chain(e, index, span, p_s, ds_s):
                rows = rows_of(index)
                size = (span + 1) * span_rows
                keys = k_s[e, :size]
                grads = heads_of(g_s, index, e)
                scores = lax.dot_general(
                    keys, heads_of(q_ref, index, e), NT, preferred_element_type=jnp.float32
                )
                last = scores[size - span_rows :] + bias
                if span:
                    last = jnp.concatenate([scores[: size - span_rows], last], axis=0)
                grad_probs = lax.dot_general(
                    v_s[e, :size], grads, NT, preferred_element_type=jnp.float32
                )
                dots = row_dots(grads, heads_of(o_ref, index, e))
                yield
                probs = softmax(last)
                grad_scores = (probs.astype(jnp.float32) * (grad_probs - dots)).astype(jnp.bfloat16)
                p_s[e, :size] = probs
                ds_s[e, :size] = grad_scores
                yield
                query_grad = jnp.dot(keys.T, grad_scores, preferred_element_type=jnp.float32)
                query_grad = query_grad.T * scale
                for r in range(repeat):
                    lanes = slice((e * repeat + r) * DH, (e * repeat + r + 1) * DH)
                    g_out_ref[rows, lanes] = (
                        g_s[rows, lanes].astype(jnp.float32)
                        + query_grad[r * span_rows : (r + 1) * span_rows]
                    ).astype(g_out_ref.dtype)
                yield

            def totals(e):
                for weights_hi, weights_lo, ref, total, factor in (
                    (p_hi, p_lo, g_s, dv_s, 1.0),
                    (ds_hi, ds_lo, q_ref, dk_s, scale),
                ):
                    right_hi = heads_of(ref, high_part, e)
                    right_lo = heads_of(ref, 1 - high_part, e)
                    near = jnp.dot(
                        jnp.concatenate([weights_hi[e, :split], weights_lo[e, :split]], axis=1),
                        jnp.concatenate([right_hi, right_lo], axis=0),
                        preferred_element_type=jnp.float32,
                    )
                    far = jnp.dot(
                        weights_hi[e, split:seen], right_hi, preferred_element_type=jnp.float32
                    )
                    total[e, :split] = near * factor
                    total[e, split:seen] = far * factor
                    if seen < total.shape[1]:
                        total[e, seen:] = jnp.zeros((total.shape[1] - seen, DH), jnp.float32)

            pending = None
            for e in range(heads):
                for one in (
                    chain(e, 1 - high_part, low, p_lo, ds_lo),
                    chain(e, high_part, high, p_hi, ds_hi),
                ):
                    next(one)
                    if pending is not None:
                        next(pending)
                        next(pending)
                    pending = one
                if e:
                    totals(e - 1)
            next(pending)
            next(pending)
            totals(heads - 1)

        for low in range(spans // 2):
            pl.when(low_span == low)(functools.partial(with_low, low))
        for out, parts in zip(outs, targets):
            for at, part in enumerate(parts):
                rows = rows_of(span_at(part))
                for e in range(heads):
                    here = (slice(at * span_rows, (at + 1) * span_rows), slice(e * DH, (e + 1) * DH))
                    out[(0, *here)] = dk_s[e, rows].astype(out.dtype)
                    out[(1, *here)] = dv_s[e, rows].astype(out.dtype)

    write_live(live, g_s, g_out_ref, outs, compute)


def general_kernel(
    slot, repeat, spans_ref, layers_ref, q_ref, g_ref, o_ref, piece, g_out_ref, out, p_s, ds_s
):
    tokens = q_ref.shape[0]
    span_rows = tokens // 2
    keys_total = p_s.shape[0]
    pair = 2 * DH
    own = lax.axis_index("ctx")

    def compute():
        keys = piece[0]
        values = piece[1]
        keys_t = keys.T
        lane = lax.broadcasted_iota(jnp.int32, (span_rows, tokens), 1)
        query_pos = jnp.where(
            lane < span_rows,
            spans_ref[2 * own] * span_rows + lane,
            (spans_ref[2 * own + 1] - 1) * span_rows + lane,
        )
        row = lax.broadcasted_iota(jnp.int32, (span_rows, tokens), 0)
        bias = jnp.concatenate(
            [
                jnp.where(spans_ref[t] * span_rows + row <= query_pos, 0.0, HIDDEN)
                for t in range(keys_total // span_rows)
            ],
            axis=0,
        )
        bias = jnp.concatenate([bias, bias], axis=1)

        @pl.loop(0, repeat // 2)
        def _(index):
            def heads_of(ref):
                return jnp.concatenate(
                    [ref[:, pl.ds(index * pair + part * DH, DH)] for part in range(2)], axis=0
                )

            grads = heads_of(g_ref)
            dots = row_dots(grads, heads_of(o_ref))
            scores = lax.dot_general(keys, heads_of(q_ref), NT, preferred_element_type=jnp.float32)
            probs = softmax(scores + bias)
            grad_probs = lax.dot_general(values, grads, NT, preferred_element_type=jnp.float32)
            grad_scores = (probs.astype(jnp.float32) * (grad_probs - dots)).astype(jnp.bfloat16)
            query_grad = jnp.dot(keys_t, grad_scores, preferred_element_type=jnp.float32)
            query_grad = query_grad.T * DH ** (-0.5)
            columns = pl.ds(index * 2 * tokens, 2 * tokens)
            p_s[:, columns] = probs
            ds_s[:, columns] = grad_scores
            for part in range(2):
                lanes = pl.ds(index * pair + part * DH, DH)
                g_out_ref[:, lanes] = (
                    g_ref[:, lanes].astype(jnp.float32)
                    + query_grad[part * tokens : (part + 1) * tokens]
                ).astype(g_out_ref.dtype)

        q_all = jnp.concatenate([q_ref[:, r * DH : (r + 1) * DH] for r in range(repeat)], axis=0)
        g_all = jnp.concatenate([g_ref[:, r * DH : (r + 1) * DH] for r in range(repeat)], axis=0)
        out[0] = jnp.dot(ds_s[...], q_all, preferred_element_type=jnp.float32) * DH ** (-0.5)
        out[1] = jnp.dot(p_s[...], g_all, preferred_element_type=jnp.float32)

    live = layers_ref[lax.axis_index("section")] > slot
    write_live(live, g_ref, g_out_ref, [out], compute)


def general_layer(slot, span_order, section_layers, queries, gradient, saved_out, piece):
    tokens, width = gradient.shape
    kv_width = piece.shape[-1]
    groups = kv_width // DH
    repeat = width // kv_width
    keys_total = piece.shape[1]
    head_block = pl.BlockSpec((None, None, tokens, repeat * DH), lambda e: (0, slot, 0, e))
    grad_block = pl.BlockSpec((tokens, repeat * DH), lambda e: (0, e))
    key_block = pl.BlockSpec((2, keys_total, DH), lambda e: (0, 0, e))
    return pl.pallas_call(
        functools.partial(general_kernel, slot, repeat),
        grid=(groups,),
        in_specs=[
            pl.BlockSpec(memory_space=pltpu.SMEM),
            pl.BlockSpec(memory_space=pltpu.SMEM),
            head_block,
            grad_block,
            head_block,
            key_block,
        ],
        out_specs=[grad_block, key_block],
        out_shape=[
            jax.ShapeDtypeStruct((tokens, width), jnp.bfloat16),
            jax.ShapeDtypeStruct((2, keys_total, kv_width), jnp.float32),
        ],
        scratch_shapes=[pltpu.VMEM((keys_total, repeat * tokens), jnp.bfloat16)] * 2,
        compiler_params=pltpu.CompilerParams(vmem_limit_bytes=48 << 20),
        name=f"layer_{slot}",
    )(span_order, section_layers, queries, gradient, saved_out, piece)


def general_device(queries, keyvals, saved_out, grad_in, section_layers, span_order):
    slots = queries.shape[1]
    gradient = grad_in[0]
    results = [None] * slots
    for slot in reversed(range(slots)):
        piece = lax.all_gather(keyvals[0, slot], "ctx", axis=1, tiled=True)
        gradient, part = general_layer(
            slot, span_order, section_layers, queries, gradient, saved_out, piece
        )
        total = lax.psum_scatter(part, "ctx", scatter_dimension=1, tiled=True)
        results[slot] = total.astype(jnp.bfloat16)
    return jnp.stack(results)[None], shifted(gradient[None], "section", -1)


WHOLES = tuple(((d, 0), (d, 1)) for d in range(4))
FULLS = (*WHOLES[:3], ((3, 0),), ((3, 1),))
HALVES = (WHOLES[0],) + tuple(((d, p),) for d in (1, 2, 3) for p in range(2))
TWO_PHASES = (WHOLES[0], ((3, 0), (1, 0)), ((3, 1), (2, 1)), ((1, 1),), ((2, 0),))
FLOAT, SHORT = jnp.float32, jnp.bfloat16


def square_layers(start, heads, meta, queries, gradient, saved_out, pieces, parts_of, targets, types):
    slots, tokens, width = queries.shape[1:]
    repeat = width // (CHUNKS[-1][1] * DH)
    half = tokens // 2
    keys_total = sum(len(parts) for parts in parts_of) * half
    lanes = heads * DH
    at = start // heads
    head_block = pl.BlockSpec(
        (None, None, tokens, repeat * lanes), lambda s: (0, slots - 1 - s, 0, at)
    )
    return pl.pallas_call(
        functools.partial(square_kernel, parts_of, targets, repeat, heads, slots),
        grid=(slots,),
        in_specs=[
            pl.BlockSpec(memory_space=pltpu.SMEM),
            head_block,
            pl.BlockSpec((tokens, repeat * lanes), lambda s: (0, 0)),
            head_block,
        ]
        + [
            pl.BlockSpec((None, 2, len(parts) * half, lanes), lambda s: (slots - 1 - s, 0, 0, 0))
            for parts in parts_of
        ],
        out_specs=[pl.BlockSpec((tokens, repeat * lanes), lambda s: (0, 0))]
        + [
            pl.BlockSpec((None, 2, len(parts) * half, lanes), lambda s: (slots - 1 - s, 0, 0, 0))
            for parts in targets
        ],
        out_shape=[jax.ShapeDtypeStruct((tokens, repeat * lanes), jnp.bfloat16)]
        + [
            jax.ShapeDtypeStruct((slots, 2, len(parts) * half, lanes), dtype)
            for parts, dtype in zip(targets, types)
        ],
        scratch_shapes=[
            pltpu.VMEM((tokens, repeat * lanes), jnp.bfloat16),
            pltpu.VMEM((heads, keys_total, DH), jnp.bfloat16),
            pltpu.VMEM((heads, keys_total, DH), jnp.bfloat16),
            pltpu.VMEM((heads, keys_total, DH), jnp.float32),
            pltpu.VMEM((heads, keys_total, DH), jnp.float32),
        ]
        + [
            pltpu.VMEM((heads, rows, repeat * half), jnp.bfloat16)
            for rows in (keys_total, keys_total // 2, keys_total, keys_total // 2)
        ],
        compiler_params=pltpu.CompilerParams(vmem_limit_bytes=48 << 20),
        cost_estimate=pl.CostEstimate(
            flops=10 * slots * tokens * repeat * lanes * keys_total,
            bytes_accessed=16 * slots * tokens * repeat * lanes,
            transcendentals=slots * tokens * repeat * heads * keys_total,
        ),
        name=f"layers_{start}",
    )(meta, queries, gradient, saved_out, *pieces)


CHUNKS = ((0, 2), (2, 4))


def on_device(queries, keyvals, saved_out, grad_in, section_layers, span_order):
    half = queries.shape[2] // 2
    if lax.axis_size("ctx") != 4 or keyvals.shape[4] != CHUNKS[-1][1] * DH:
        return general_device(queries, keyvals, saved_out, grad_in, section_layers, span_order)

    meta = jnp.concatenate([span_order, section_layers])

    def block_of(chunk, after):
        start, stop = chunk
        own = keyvals[0, :, :, :, start * DH : stop * DH]
        if after:
            own, _ = lax.optimization_barrier((own, after))
        return own

    def by_halves(own):
        low = own[:, :, :half]
        high = own[:, :, half:]
        x_high = exchanged(high, "ctx", 1)
        x_low = exchanged(low, "ctx", 1)
        y_low = exchanged(low, "ctx", 2)
        y_high = exchanged(high, "ctx", 2)
        far_high = exchanged(x_high, "ctx", 2)
        far_low = exchanged(y_low, "ctx", 1)
        return [own, x_low, x_high, y_low, y_high, far_low, far_high], HALVES

    def direct(own):
        return [own] + [exchanged(own, "ctx", mask) for mask in (1, 2, 3)], WHOLES

    def two_phases(mine, first_x, first_y, rest_x, rest_y):
        got_x = exchanged(first_x, "ctx", 1)
        got_y = exchanged(first_y, "ctx", 2)
        second_x = (rest_x + got_y[:, :, :half].astype(FLOAT)).astype(SHORT)
        second_y = (rest_y + got_x[:, :, :half].astype(FLOAT)).astype(SHORT)
        more_x = exchanged(second_x, "ctx", 1)
        more_y = exchanged(second_y, "ctx", 2)
        low = mine[:, :, :half] + got_x[:, :, half:].astype(FLOAT) + more_y.astype(FLOAT)
        high = mine[:, :, half:] + got_y[:, :, half:].astype(FLOAT) + more_x.astype(FLOAT)
        return jnp.concatenate([low, high], axis=2).astype(SHORT)

    gathers = [by_halves, direct]
    pieces = []
    for at, chunk in enumerate(CHUNKS):
        after = []
        if at == 1:
            after = [pieces[0][0][i] for i in (2,)]
        pieces.append(gathers[at](block_of(chunk, after)))
    repeat = queries.shape[3] // keyvals.shape[4]

    def columns(array, start, stop):
        return array[..., start * repeat * DH : stop * repeat * DH]

    key_parts = []
    down_parts = []
    results = []
    for (start, stop), (own_pieces, parts_of), how in zip(CHUNKS, pieces, [(TWO_PHASES, (FLOAT, SHORT, SHORT, FLOAT, FLOAT), two_phases), (TWO_PHASES, (FLOAT, SHORT, SHORT, FLOAT, FLOAT), two_phases)]):
        targets, types, join = how
        gradient, *parts = square_layers(
            start, stop - start, meta, queries, columns(grad_in[0], start, stop), saved_out, own_pieces, parts_of, targets, types
        )
        results.append(gradient)
        key_parts.append(join(*parts))
    down_parts = [shifted(result, "section", -1) for result in results]
    grad_kv = jnp.concatenate(key_parts, axis=3)[None]
    grad_down = jnp.concatenate(down_parts, axis=1)[None]
    return (grad_kv, grad_down)


def solution(mesh):
    in_specs = (
        P("section", None, "ctx", None),
        P("section", None, None, "ctx", None),
        P("section", None, "ctx", None),
        P("section", "ctx", None),
        P(),
        P(),
    )
    out_specs = (P("section", None, None, "ctx", None), P("section", "ctx", None))
    return jax.shard_map(
        on_device, mesh=mesh, in_specs=in_specs, out_specs=out_specs, check_vma=False
    )
```

```python
import functools
import math

import jax
import jax.numpy as jnp
from jax import lax
from jax.experimental import pallas as pl
from jax.experimental.pallas import tpu as pltpu
from jax.sharding import PartitionSpec as P

DH = 128
HIDDEN = -1e30
NT = (((1,), (1,)), ((), ()))


def exchanged(array, axis, mask):
    length = lax.axis_size(axis)
    return lax.ppermute(array, axis, [(i, i ^ mask) for i in range(length)])


def shifted(array, axis, by):
    length = lax.axis_size(axis)
    return lax.ppermute(array, axis, [(i, (i + by) % length) for i in range(length)])


def write_live(live, g_ref, g_out_ref, outs, compute):
    @pl.when(jnp.logical_not(live))
    def _():
        g_out_ref[...] = g_ref[...]
        for out in outs:
            out[...] = jnp.zeros_like(out)

    pl.when(live)(compute)


def row_dots(grads, outputs):
    product = grads.astype(jnp.float32) * outputs.astype(jnp.float32)
    return jnp.sum(product.T, axis=0, keepdims=True)


def softmax(scores):
    factor = DH ** (-0.5) * math.log2(math.e)
    top = jnp.max(scores, axis=0, keepdims=True)
    powers = jnp.exp2(scores * factor - top * factor)
    inverse = 1.0 / jnp.sum(powers, axis=0, keepdims=True)
    return (powers * inverse).astype(jnp.bfloat16)


def square_kernel(parts_of, targets, repeat, heads, slots, meta_ref, q_ref, g_ref, o_ref, *refs):
    pieces = refs[: len(parts_of)]
    g_out_ref = refs[len(parts_of)]
    outs = refs[len(parts_of) + 1 : len(parts_of) + 1 + len(targets)]
    g_s, k_s, v_s, dk_s, dv_s, p_hi, p_lo, ds_hi, ds_lo = refs[-9:]
    step = pl.program_id(0)
    live = meta_ref[k_s.shape[1] // (q_ref.shape[0] // 2) + lax.axis_index("section")] > slots - 1 - step
    span_rows = q_ref.shape[0] // 2
    spans = k_s.shape[1] // span_rows
    scale = DH ** (-0.5)
    own = lax.axis_index("ctx")

    @pl.when(step == 0)
    def _():
        g_s[...] = g_ref[...]

    @pl.when(step != 0)
    def _():
        g_s[...] = g_out_ref[...]

    def span_at(part):
        return meta_ref[2 * (own ^ part[0]) + part[1]]

    def rows_of(index):
        return pl.ds(pl.multiple_of(index * span_rows, span_rows), span_rows)

    def compute():
        for piece, parts in zip(pieces, parts_of):
            for at, part in enumerate(parts):
                rows = rows_of(span_at(part))
                for e in range(heads):
                    here = (slice(at * span_rows, (at + 1) * span_rows), slice(e * DH, (e + 1) * DH))
                    k_s[e, rows] = piece[(0, *here)]
                    v_s[e, rows] = piece[(1, *here)]
        first, second = meta_ref[2 * own], meta_ref[2 * own + 1]
        low_span = jnp.minimum(first, second)
        high_part = (second > first).astype(jnp.int32)

        def with_low(low):
            high = spans - 1 - low
            seen = (high + 1) * span_rows
            split = (low + 1) * span_rows
            shape = (span_rows, repeat * span_rows)
            offset = lax.rem(lax.broadcasted_iota(jnp.int32, shape, 1), span_rows)
            bias = jnp.where(lax.broadcasted_iota(jnp.int32, shape, 0) <= offset, 0.0, HIDDEN)

            def heads_of(ref, index, e):
                rows = rows_of(index)
                return jnp.concatenate(
                    [ref[rows, (e * repeat + r) * DH : (e * repeat + r + 1) * DH] for r in range(repeat)],
                    axis=0,
                )

            def chain(e, index, span, p_s, ds_s):
                rows = rows_of(index)
                size = (span + 1) * span_rows
                keys = k_s[e, :size]
                grads = heads_of(g_s, index, e)
                scores = lax.dot_general(
                    keys, heads_of(q_ref, index, e), NT, preferred_element_type=jnp.float32
                )
                last = scores[size - span_rows :] + bias
                if span:
                    last = jnp.concatenate([scores[: size - span_rows], last], axis=0)
                grad_probs = lax.dot_general(
                    v_s[e, :size], grads, NT, preferred_element_type=jnp.float32
                )
                dots = row_dots(grads, heads_of(o_ref, index, e))
                yield
                probs = softmax(last)
                grad_scores = (probs.astype(jnp.float32) * (grad_probs - dots)).astype(jnp.bfloat16)
                p_s[e, :size] = probs
                ds_s[e, :size] = grad_scores
                yield
                query_grad = jnp.dot(keys.T, grad_scores, preferred_element_type=jnp.float32)
                query_grad = query_grad.T * scale
                for r in range(repeat):
                    lanes = slice((e * repeat + r) * DH, (e * repeat + r + 1) * DH)
                    g_out_ref[rows, lanes] = (
                        g_s[rows, lanes].astype(jnp.float32)
                        + query_grad[r * span_rows : (r + 1) * span_rows]
                    ).astype(g_out_ref.dtype)
                yield

            def totals(e):
                for weights_hi, weights_lo, ref, total, factor in (
                    (p_hi, p_lo, g_s, dv_s, 1.0),
                    (ds_hi, ds_lo, q_ref, dk_s, scale),
                ):
                    right_hi = heads_of(ref, high_part, e)
                    right_lo = heads_of(ref, 1 - high_part, e)
                    near = jnp.dot(
                        jnp.concatenate([weights_hi[e, :split], weights_lo[e, :split]], axis=1),
                        jnp.concatenate([right_hi, right_lo], axis=0),
                        preferred_element_type=jnp.float32,
                    )
                    far = jnp.dot(
                        weights_hi[e, split:seen], right_hi, preferred_element_type=jnp.float32
                    )
                    total[e, :split] = near * factor
                    total[e, split:seen] = far * factor
                    if seen < total.shape[1]:
                        total[e, seen:] = jnp.zeros((total.shape[1] - seen, DH), jnp.float32)

            pending = None
            for e in range(heads):
                for one in (
                    chain(e, 1 - high_part, low, p_lo, ds_lo),
                    chain(e, high_part, high, p_hi, ds_hi),
                ):
                    next(one)
                    if pending is not None:
                        next(pending)
                        next(pending)
                    pending = one
                if e:
                    totals(e - 1)
            next(pending)
            next(pending)
            totals(heads - 1)

        for low in range(spans // 2):
            pl.when(low_span == low)(functools.partial(with_low, low))
        for out, parts in zip(outs, targets):
            for at, part in enumerate(parts):
                rows = rows_of(span_at(part))
                for e in range(heads):
                    here = (slice(at * span_rows, (at + 1) * span_rows), slice(e * DH, (e + 1) * DH))
                    out[(0, *here)] = dk_s[e, rows].astype(out.dtype)
                    out[(1, *here)] = dv_s[e, rows].astype(out.dtype)

    write_live(live, g_s, g_out_ref, outs, compute)


def general_kernel(
    slot, repeat, spans_ref, layers_ref, q_ref, g_ref, o_ref, piece, g_out_ref, out, p_s, ds_s
):
    tokens = q_ref.shape[0]
    span_rows = tokens // 2
    keys_total = p_s.shape[0]
    pair = 2 * DH
    own = lax.axis_index("ctx")

    def compute():
        keys = piece[0]
        values = piece[1]
        keys_t = keys.T
        lane = lax.broadcasted_iota(jnp.int32, (span_rows, tokens), 1)
        query_pos = jnp.where(
            lane < span_rows,
            spans_ref[2 * own] * span_rows + lane,
            (spans_ref[2 * own + 1] - 1) * span_rows + lane,
        )
        row = lax.broadcasted_iota(jnp.int32, (span_rows, tokens), 0)
        bias = jnp.concatenate(
            [
                jnp.where(spans_ref[t] * span_rows + row <= query_pos, 0.0, HIDDEN)
                for t in range(keys_total // span_rows)
            ],
            axis=0,
        )
        bias = jnp.concatenate([bias, bias], axis=1)

        @pl.loop(0, repeat // 2)
        def _(index):
            def heads_of(ref):
                return jnp.concatenate(
                    [ref[:, pl.ds(index * pair + part * DH, DH)] for part in range(2)], axis=0
                )

            grads = heads_of(g_ref)
            dots = row_dots(grads, heads_of(o_ref))
            scores = lax.dot_general(keys, heads_of(q_ref), NT, preferred_element_type=jnp.float32)
            probs = softmax(scores + bias)
            grad_probs = lax.dot_general(values, grads, NT, preferred_element_type=jnp.float32)
            grad_scores = (probs.astype(jnp.float32) * (grad_probs - dots)).astype(jnp.bfloat16)
            query_grad = jnp.dot(keys_t, grad_scores, preferred_element_type=jnp.float32)
            query_grad = query_grad.T * DH ** (-0.5)
            columns = pl.ds(index * 2 * tokens, 2 * tokens)
            p_s[:, columns] = probs
            ds_s[:, columns] = grad_scores
            for part in range(2):
                lanes = pl.ds(index * pair + part * DH, DH)
                g_out_ref[:, lanes] = (
                    g_ref[:, lanes].astype(jnp.float32)
                    + query_grad[part * tokens : (part + 1) * tokens]
                ).astype(g_out_ref.dtype)

        q_all = jnp.concatenate([q_ref[:, r * DH : (r + 1) * DH] for r in range(repeat)], axis=0)
        g_all = jnp.concatenate([g_ref[:, r * DH : (r + 1) * DH] for r in range(repeat)], axis=0)
        out[0] = jnp.dot(ds_s[...], q_all, preferred_element_type=jnp.float32) * DH ** (-0.5)
        out[1] = jnp.dot(p_s[...], g_all, preferred_element_type=jnp.float32)

    live = layers_ref[lax.axis_index("section")] > slot
    write_live(live, g_ref, g_out_ref, [out], compute)


def general_layer(slot, span_order, section_layers, queries, gradient, saved_out, piece):
    tokens, width = gradient.shape
    kv_width = piece.shape[-1]
    groups = kv_width // DH
    repeat = width // kv_width
    keys_total = piece.shape[1]
    head_block = pl.BlockSpec((None, None, tokens, repeat * DH), lambda e: (0, slot, 0, e))
    grad_block = pl.BlockSpec((tokens, repeat * DH), lambda e: (0, e))
    key_block = pl.BlockSpec((2, keys_total, DH), lambda e: (0, 0, e))
    return pl.pallas_call(
        functools.partial(general_kernel, slot, repeat),
        grid=(groups,),
        in_specs=[
            pl.BlockSpec(memory_space=pltpu.SMEM),
            pl.BlockSpec(memory_space=pltpu.SMEM),
            head_block,
            grad_block,
            head_block,
            key_block,
        ],
        out_specs=[grad_block, key_block],
        out_shape=[
            jax.ShapeDtypeStruct((tokens, width), jnp.bfloat16),
            jax.ShapeDtypeStruct((2, keys_total, kv_width), jnp.float32),
        ],
        scratch_shapes=[pltpu.VMEM((keys_total, repeat * tokens), jnp.bfloat16)] * 2,
        compiler_params=pltpu.CompilerParams(vmem_limit_bytes=48 << 20),
        name=f"layer_{slot}",
    )(span_order, section_layers, queries, gradient, saved_out, piece)


def general_device(queries, keyvals, saved_out, grad_in, section_layers, span_order):
    slots = queries.shape[1]
    gradient = grad_in[0]
    results = [None] * slots
    for slot in reversed(range(slots)):
        piece = lax.all_gather(keyvals[0, slot], "ctx", axis=1, tiled=True)
        gradient, part = general_layer(
            slot, span_order, section_layers, queries, gradient, saved_out, piece
        )
        total = lax.psum_scatter(part, "ctx", scatter_dimension=1, tiled=True)
        results[slot] = total.astype(jnp.bfloat16)
    return jnp.stack(results)[None], shifted(gradient[None], "section", -1)


WHOLES = tuple(((d, 0), (d, 1)) for d in range(4))
FULLS = (*WHOLES[:3], ((3, 0),), ((3, 1),))
HALVES = (WHOLES[0],) + tuple(((d, p),) for d in (1, 2, 3) for p in range(2))
TWO_PHASES = (WHOLES[0], ((3, 0), (1, 0)), ((3, 1), (2, 1)), ((1, 1),), ((2, 0),))
FLOAT, SHORT = jnp.float32, jnp.bfloat16


def square_layers(start, heads, meta, queries, gradient, saved_out, pieces, parts_of, targets, types):
    slots, tokens, width = queries.shape
    repeat = gradient.shape[1] // (heads * DH)
    half = tokens // 2
    keys_total = sum(len(parts) for parts in parts_of) * half
    lanes = heads * DH
    offset = start // heads if width > gradient.shape[1] else 0
    head_block = pl.BlockSpec(
        (None, tokens, repeat * lanes), lambda s: (slots - 1 - s, 0, offset)
    )
    return pl.pallas_call(
        functools.partial(square_kernel, parts_of, targets, repeat, heads, slots),
        grid=(slots,),
        in_specs=[
            pl.BlockSpec(memory_space=pltpu.SMEM),
            head_block,
            pl.BlockSpec((tokens, repeat * lanes), lambda s: (0, 0)),
            head_block,
        ]
        + [
            pl.BlockSpec((None, 2, len(parts) * half, lanes), lambda s: (slots - 1 - s, 0, 0, 0))
            for parts in parts_of
        ],
        out_specs=[pl.BlockSpec((tokens, repeat * lanes), lambda s: (0, 0))]
        + [
            pl.BlockSpec((None, 2, len(parts) * half, lanes), lambda s: (slots - 1 - s, 0, 0, 0))
            for parts in targets
        ],
        out_shape=[jax.ShapeDtypeStruct((tokens, repeat * lanes), jnp.bfloat16)]
        + [
            jax.ShapeDtypeStruct((slots, 2, len(parts) * half, lanes), dtype)
            for parts, dtype in zip(targets, types)
        ],
        scratch_shapes=[
            pltpu.VMEM((tokens, repeat * lanes), jnp.bfloat16),
            pltpu.VMEM((heads, keys_total, DH), jnp.bfloat16),
            pltpu.VMEM((heads, keys_total, DH), jnp.bfloat16),
            pltpu.VMEM((heads, keys_total, DH), jnp.float32),
            pltpu.VMEM((heads, keys_total, DH), jnp.float32),
        ]
        + [
            pltpu.VMEM((heads, rows, repeat * half), jnp.bfloat16)
            for rows in (keys_total, keys_total // 2, keys_total, keys_total // 2)
        ],
        compiler_params=pltpu.CompilerParams(vmem_limit_bytes=48 << 20),
        cost_estimate=pl.CostEstimate(
            flops=10 * slots * tokens * repeat * lanes * keys_total,
            bytes_accessed=16 * slots * tokens * repeat * lanes,
            transcendentals=slots * tokens * repeat * heads * keys_total,
        ),
        name=f"layers_{start}",
    )(meta, queries, gradient, saved_out, *pieces)


CHUNKS = ((0, 2), (2, 4))


def on_device(queries, keyvals, saved_out, grad_in, section_layers, span_order):
    half = queries.shape[2] // 2
    if lax.axis_size("ctx") != 4 or keyvals.shape[4] != CHUNKS[-1][1] * DH:
        return general_device(queries, keyvals, saved_out, grad_in, section_layers, span_order)

    meta = jnp.concatenate([span_order, section_layers])

    def block_of(chunk, after):
        start, stop = chunk
        own = keyvals[0, :, :, :, start * DH : stop * DH]
        if after:
            own, _ = lax.optimization_barrier((own, after))
        return own

    def by_halves(own):
        low = own[:, :, :half]
        high = own[:, :, half:]
        x_high = exchanged(high, "ctx", 1)
        x_low = exchanged(low, "ctx", 1)
        y_low = exchanged(low, "ctx", 2)
        y_high = exchanged(high, "ctx", 2)
        far_high = exchanged(x_high, "ctx", 2)
        far_low = exchanged(y_low, "ctx", 1)
        return [own, x_low, x_high, y_low, y_high, far_low, far_high], HALVES

    def direct(own):
        return [own] + [exchanged(own, "ctx", mask) for mask in (1, 2, 3)], WHOLES

    def two_phases(mine, first_x, first_y, rest_x, rest_y, tail=None):
        got_x = exchanged(first_x, "ctx", 1)
        got_y = exchanged(first_y, "ctx", 2)
        second_x = (rest_x + got_y[:, :, :half].astype(FLOAT)).astype(SHORT)
        second_y = (rest_y + got_x[:, :, :half].astype(FLOAT)).astype(SHORT)
        more_x = exchanged(second_x, "ctx", 1)
        more_y = exchanged(second_y, "ctx", 2)
        if tail is not None:
            more_x, tail = lax.optimization_barrier((more_x, tail))
        low = mine[:, :, :half] + got_x[:, :, half:].astype(FLOAT) + more_y.astype(FLOAT)
        high = mine[:, :, half:] + got_y[:, :, half:].astype(FLOAT) + more_x.astype(FLOAT)
        total = jnp.concatenate([low, high], axis=2).astype(SHORT)
        return total if tail is None else (total, tail)

    gathers = [by_halves, direct]
    pieces = []
    for at, chunk in enumerate(CHUNKS):
        after = []
        if at == 1:
            after = [pieces[0][0][i] for i in (2,)]
        pieces.append(gathers[at](block_of(chunk, after)))
    repeat = queries.shape[3] // keyvals.shape[4]

    def columns(array, start, stop):
        return array[..., start * repeat * DH : stop * repeat * DH]

    key_parts = []
    down_parts = []
    for (start, stop), (own_pieces, parts_of), how in zip(CHUNKS, pieces, [(TWO_PHASES, (FLOAT, SHORT, SHORT, FLOAT, FLOAT), two_phases), (TWO_PHASES, (FLOAT, SHORT, SHORT, FLOAT, FLOAT), two_phases)]):
        targets, types, join = how
        asked, saved = queries[0], saved_out[0]
        if start:
            asked, saved = columns(asked, start, stop), columns(saved, start, stop)
            asked, saved, gradient = lax.optimization_barrier((asked, saved, gradient))
        gradient, *parts = square_layers(
            start, stop - start, meta, asked, columns(grad_in[0], start, stop), saved, own_pieces, parts_of, targets, types
        )
        down_parts.append(shifted(gradient, "section", -1))
        if stop == CHUNKS[-1][1]:
            grad_down = jnp.concatenate(down_parts, axis=1)[None]
            result, grad_down = join(*parts, tail=grad_down)
        else:
            result = join(*parts)
        key_parts.append(result)
    grad_kv = jnp.concatenate(key_parts, axis=3)[None]
    return (grad_kv, grad_down)


def solution(mesh):
    in_specs = (
        P("section", None, "ctx", None),
        P("section", None, None, "ctx", None),
        P("section", None, "ctx", None),
        P("section", "ctx", None),
        P(),
        P(),
    )
    out_specs = (P("section", None, None, "ctx", None), P("section", "ctx", None))
    return jax.shard_map(
        on_device, mesh=mesh, in_specs=in_specs, out_specs=out_specs, check_vma=False
    )
```

```python
import functools
import math

import jax
import jax.numpy as jnp
from jax import lax
from jax.experimental import pallas as pl
from jax.experimental.pallas import tpu as pltpu
from jax.sharding import PartitionSpec as P

DH = 128
HIDDEN = -1e30
NT = (((1,), (1,)), ((), ()))


def exchanged(array, axis, mask):
    length = lax.axis_size(axis)
    return lax.ppermute(array, axis, [(i, i ^ mask) for i in range(length)])


def shifted(array, axis, by):
    length = lax.axis_size(axis)
    return lax.ppermute(array, axis, [(i, (i + by) % length) for i in range(length)])


def write_live(live, g_ref, g_out_ref, outs, compute):
    @pl.when(jnp.logical_not(live))
    def _():
        g_out_ref[...] = g_ref[...]
        for out in outs:
            out[...] = jnp.zeros_like(out)

    pl.when(live)(compute)


def row_dots(grads, outputs):
    product = grads.astype(jnp.float32) * outputs.astype(jnp.float32)
    return jnp.sum(product.T, axis=0, keepdims=True)


def softmax(scores):
    factor = DH ** (-0.5) * math.log2(math.e)
    top = jnp.max(scores, axis=0, keepdims=True)
    powers = jnp.exp2(scores * factor - top * factor)
    inverse = 1.0 / jnp.sum(powers, axis=0, keepdims=True)
    return (powers * inverse).astype(jnp.bfloat16)


def square_kernel(parts_of, targets, repeat, heads, slots, meta_ref, q_ref, g_ref, o_ref, *refs):
    pieces = refs[: len(parts_of)]
    g_out_ref = refs[len(parts_of)]
    outs = refs[len(parts_of) + 1 : len(parts_of) + 1 + len(targets)]
    g_s, k_s, v_s, dk_s, dv_s, p_hi, p_lo, ds_hi, ds_lo = refs[-9:]
    step = pl.program_id(0)
    live = meta_ref[k_s.shape[1] // (q_ref.shape[0] // 2) + lax.axis_index("section")] > slots - 1 - step
    span_rows = q_ref.shape[0] // 2
    spans = k_s.shape[1] // span_rows
    scale = DH ** (-0.5)
    own = lax.axis_index("ctx")

    @pl.when(step == 0)
    def _():
        g_s[...] = g_ref[...]

    @pl.when(step != 0)
    def _():
        g_s[...] = g_out_ref[...]

    def span_at(part):
        return meta_ref[2 * (own ^ part[0]) + part[1]]

    def rows_of(index):
        return pl.ds(pl.multiple_of(index * span_rows, span_rows), span_rows)

    def compute():
        for piece, parts in zip(pieces, parts_of):
            for at, part in enumerate(parts):
                rows = rows_of(span_at(part))
                for e in range(heads):
                    here = (slice(at * span_rows, (at + 1) * span_rows), slice(e * DH, (e + 1) * DH))
                    k_s[e, rows] = piece[(0, *here)]
                    v_s[e, rows] = piece[(1, *here)]
        first, second = meta_ref[2 * own], meta_ref[2 * own + 1]
        low_span = jnp.minimum(first, second)
        high_part = (second > first).astype(jnp.int32)

        def with_low(low):
            high = spans - 1 - low
            seen = (high + 1) * span_rows
            split = (low + 1) * span_rows
            shape = (span_rows, repeat * span_rows)
            offset = lax.rem(lax.broadcasted_iota(jnp.int32, shape, 1), span_rows)
            bias = jnp.where(lax.broadcasted_iota(jnp.int32, shape, 0) <= offset, 0.0, HIDDEN)

            def heads_of(ref, index, e):
                rows = rows_of(index)
                return jnp.concatenate(
                    [ref[rows, (e * repeat + r) * DH : (e * repeat + r + 1) * DH] for r in range(repeat)],
                    axis=0,
                )

            def chain(e, index, span, p_s, ds_s):
                rows = rows_of(index)
                size = (span + 1) * span_rows
                keys = k_s[e, :size]
                grads = heads_of(g_s, index, e)
                scores = lax.dot_general(
                    keys, heads_of(q_ref, index, e), NT, preferred_element_type=jnp.float32
                )
                last = scores[size - span_rows :] + bias
                if span:
                    last = jnp.concatenate([scores[: size - span_rows], last], axis=0)
                grad_probs = lax.dot_general(
                    v_s[e, :size], grads, NT, preferred_element_type=jnp.float32
                )
                dots = row_dots(grads, heads_of(o_ref, index, e))
                yield
                probs = softmax(last)
                grad_scores = (probs.astype(jnp.float32) * (grad_probs - dots)).astype(jnp.bfloat16)
                p_s[e, :size] = probs
                ds_s[e, :size] = grad_scores
                yield
                query_grad = jnp.dot(keys.T, grad_scores, preferred_element_type=jnp.float32)
                query_grad = query_grad.T * scale
                for r in range(repeat):
                    lanes = slice((e * repeat + r) * DH, (e * repeat + r + 1) * DH)
                    g_out_ref[rows, lanes] = (
                        g_s[rows, lanes].astype(jnp.float32)
                        + query_grad[r * span_rows : (r + 1) * span_rows]
                    ).astype(g_out_ref.dtype)
                yield

            def totals(e):
                for weights_hi, weights_lo, ref, total, factor in (
                    (p_hi, p_lo, g_s, dv_s, 1.0),
                    (ds_hi, ds_lo, q_ref, dk_s, scale),
                ):
                    right_hi = heads_of(ref, high_part, e)
                    right_lo = heads_of(ref, 1 - high_part, e)
                    near = jnp.dot(
                        jnp.concatenate([weights_hi[e, :split], weights_lo[e, :split]], axis=1),
                        jnp.concatenate([right_hi, right_lo], axis=0),
                        preferred_element_type=jnp.float32,
                    )
                    far = jnp.dot(
                        weights_hi[e, split:seen], right_hi, preferred_element_type=jnp.float32
                    )
                    total[e, :split] = near * factor
                    total[e, split:seen] = far * factor
                    if seen < total.shape[1]:
                        total[e, seen:] = jnp.zeros((total.shape[1] - seen, DH), jnp.float32)

            pending = None
            for e in range(heads):
                for one in (
                    chain(e, 1 - high_part, low, p_lo, ds_lo),
                    chain(e, high_part, high, p_hi, ds_hi),
                ):
                    next(one)
                    if pending is not None:
                        next(pending)
                        next(pending)
                    pending = one
                if e:
                    totals(e - 1)
            next(pending)
            next(pending)
            totals(heads - 1)

        for low in range(spans // 2):
            pl.when(low_span == low)(functools.partial(with_low, low))
        for out, parts in zip(outs, targets):
            for at, part in enumerate(parts):
                rows = rows_of(span_at(part))
                for e in range(heads):
                    here = (slice(at * span_rows, (at + 1) * span_rows), slice(e * DH, (e + 1) * DH))
                    out[(0, *here)] = dk_s[e, rows].astype(out.dtype)
                    out[(1, *here)] = dv_s[e, rows].astype(out.dtype)

    write_live(live, g_s, g_out_ref, outs, compute)


def general_kernel(
    slot, repeat, spans_ref, layers_ref, q_ref, g_ref, o_ref, piece, g_out_ref, out, p_s, ds_s
):
    tokens = q_ref.shape[0]
    span_rows = tokens // 2
    keys_total = p_s.shape[0]
    pair = 2 * DH
    own = lax.axis_index("ctx")

    def compute():
        keys = piece[0]
        values = piece[1]
        keys_t = keys.T
        lane = lax.broadcasted_iota(jnp.int32, (span_rows, tokens), 1)
        query_pos = jnp.where(
            lane < span_rows,
            spans_ref[2 * own] * span_rows + lane,
            (spans_ref[2 * own + 1] - 1) * span_rows + lane,
        )
        row = lax.broadcasted_iota(jnp.int32, (span_rows, tokens), 0)
        bias = jnp.concatenate(
            [
                jnp.where(spans_ref[t] * span_rows + row <= query_pos, 0.0, HIDDEN)
                for t in range(keys_total // span_rows)
            ],
            axis=0,
        )
        bias = jnp.concatenate([bias, bias], axis=1)

        @pl.loop(0, repeat // 2)
        def _(index):
            def heads_of(ref):
                return jnp.concatenate(
                    [ref[:, pl.ds(index * pair + part * DH, DH)] for part in range(2)], axis=0
                )

            grads = heads_of(g_ref)
            dots = row_dots(grads, heads_of(o_ref))
            scores = lax.dot_general(keys, heads_of(q_ref), NT, preferred_element_type=jnp.float32)
            probs = softmax(scores + bias)
            grad_probs = lax.dot_general(values, grads, NT, preferred_element_type=jnp.float32)
            grad_scores = (probs.astype(jnp.float32) * (grad_probs - dots)).astype(jnp.bfloat16)
            query_grad = jnp.dot(keys_t, grad_scores, preferred_element_type=jnp.float32)
            query_grad = query_grad.T * DH ** (-0.5)
            columns = pl.ds(index * 2 * tokens, 2 * tokens)
            p_s[:, columns] = probs
            ds_s[:, columns] = grad_scores
            for part in range(2):
                lanes = pl.ds(index * pair + part * DH, DH)
                g_out_ref[:, lanes] = (
                    g_ref[:, lanes].astype(jnp.float32)
                    + query_grad[part * tokens : (part + 1) * tokens]
                ).astype(g_out_ref.dtype)

        q_all = jnp.concatenate([q_ref[:, r * DH : (r + 1) * DH] for r in range(repeat)], axis=0)
        g_all = jnp.concatenate([g_ref[:, r * DH : (r + 1) * DH] for r in range(repeat)], axis=0)
        out[0] = jnp.dot(ds_s[...], q_all, preferred_element_type=jnp.float32) * DH ** (-0.5)
        out[1] = jnp.dot(p_s[...], g_all, preferred_element_type=jnp.float32)

    live = layers_ref[lax.axis_index("section")] > slot
    write_live(live, g_ref, g_out_ref, [out], compute)


def general_layer(slot, span_order, section_layers, queries, gradient, saved_out, piece):
    tokens, width = gradient.shape
    kv_width = piece.shape[-1]
    groups = kv_width // DH
    repeat = width // kv_width
    keys_total = piece.shape[1]
    head_block = pl.BlockSpec((None, None, tokens, repeat * DH), lambda e: (0, slot, 0, e))
    grad_block = pl.BlockSpec((tokens, repeat * DH), lambda e: (0, e))
    key_block = pl.BlockSpec((2, keys_total, DH), lambda e: (0, 0, e))
    return pl.pallas_call(
        functools.partial(general_kernel, slot, repeat),
        grid=(groups,),
        in_specs=[
            pl.BlockSpec(memory_space=pltpu.SMEM),
            pl.BlockSpec(memory_space=pltpu.SMEM),
            head_block,
            grad_block,
            head_block,
            key_block,
        ],
        out_specs=[grad_block, key_block],
        out_shape=[
            jax.ShapeDtypeStruct((tokens, width), jnp.bfloat16),
            jax.ShapeDtypeStruct((2, keys_total, kv_width), jnp.float32),
        ],
        scratch_shapes=[pltpu.VMEM((keys_total, repeat * tokens), jnp.bfloat16)] * 2,
        compiler_params=pltpu.CompilerParams(vmem_limit_bytes=48 << 20),
        name=f"layer_{slot}",
    )(span_order, section_layers, queries, gradient, saved_out, piece)


def general_device(queries, keyvals, saved_out, grad_in, section_layers, span_order):
    slots = queries.shape[1]
    gradient = grad_in[0]
    results = [None] * slots
    for slot in reversed(range(slots)):
        piece = lax.all_gather(keyvals[0, slot], "ctx", axis=1, tiled=True)
        gradient, part = general_layer(
            slot, span_order, section_layers, queries, gradient, saved_out, piece
        )
        total = lax.psum_scatter(part, "ctx", scatter_dimension=1, tiled=True)
        results[slot] = total.astype(jnp.bfloat16)
    return jnp.stack(results)[None], shifted(gradient[None], "section", -1)


WHOLES = tuple(((d, 0), (d, 1)) for d in range(4))
FULLS = (*WHOLES[:3], ((3, 0),), ((3, 1),))
HALVES = (WHOLES[0],) + tuple(((d, p),) for d in (1, 2, 3) for p in range(2))
TWO_PHASES = (WHOLES[0], ((3, 0), (1, 0)), ((3, 1), (2, 1)), ((1, 1),), ((2, 0),))
FLOAT, SHORT = jnp.float32, jnp.bfloat16


def square_layers(start, heads, meta, queries, gradient, saved_out, pieces, parts_of, targets, types):
    slots, tokens, width = queries.shape
    repeat = gradient.shape[1] // (heads * DH)
    half = tokens // 2
    keys_total = sum(len(parts) for parts in parts_of) * half
    lanes = heads * DH
    offset = start // heads if width > gradient.shape[1] else 0
    head_block = pl.BlockSpec(
        (None, tokens, repeat * lanes), lambda s: (slots - 1 - s, 0, offset)
    )
    return pl.pallas_call(
        functools.partial(square_kernel, parts_of, targets, repeat, heads, slots),
        grid=(slots,),
        in_specs=[
            pl.BlockSpec(memory_space=pltpu.SMEM),
            head_block,
            pl.BlockSpec((tokens, repeat * lanes), lambda s: (0, 0)),
            head_block,
        ]
        + [
            pl.BlockSpec((None, 2, len(parts) * half, lanes), lambda s: (slots - 1 - s, 0, 0, 0))
            for parts in parts_of
        ],
        out_specs=[pl.BlockSpec((tokens, repeat * lanes), lambda s: (0, 0))]
        + [
            pl.BlockSpec((None, 2, len(parts) * half, lanes), lambda s: (slots - 1 - s, 0, 0, 0))
            for parts in targets
        ],
        out_shape=[jax.ShapeDtypeStruct((tokens, repeat * lanes), jnp.bfloat16)]
        + [
            jax.ShapeDtypeStruct((slots, 2, len(parts) * half, lanes), dtype)
            for parts, dtype in zip(targets, types)
        ],
        scratch_shapes=[
            pltpu.VMEM((tokens, repeat * lanes), jnp.bfloat16),
            pltpu.VMEM((heads, keys_total, DH), jnp.bfloat16),
            pltpu.VMEM((heads, keys_total, DH), jnp.bfloat16),
            pltpu.VMEM((heads, keys_total, DH), jnp.float32),
            pltpu.VMEM((heads, keys_total, DH), jnp.float32),
        ]
        + [
            pltpu.VMEM((heads, rows, repeat * half), jnp.bfloat16)
            for rows in (keys_total, keys_total // 2, keys_total, keys_total // 2)
        ],
        compiler_params=pltpu.CompilerParams(vmem_limit_bytes=48 << 20),
        cost_estimate=pl.CostEstimate(
            flops=10 * slots * tokens * repeat * lanes * keys_total,
            bytes_accessed=16 * slots * tokens * repeat * lanes,
            transcendentals=slots * tokens * repeat * heads * keys_total,
        ),
        name=f"layers_{start}",
    )(meta, queries, gradient, saved_out, *pieces)


CHUNKS = ((0, 2), (2, 4))


def on_device(queries, keyvals, saved_out, grad_in, section_layers, span_order):
    half = queries.shape[2] // 2
    if lax.axis_size("ctx") != 4 or keyvals.shape[4] != CHUNKS[-1][1] * DH:
        return general_device(queries, keyvals, saved_out, grad_in, section_layers, span_order)

    meta = jnp.concatenate([span_order, section_layers])

    def block_of(chunk, after):
        start, stop = chunk
        own = keyvals[0, :, :, :, start * DH : stop * DH]
        if after:
            own, _ = lax.optimization_barrier((own, after))
        return own

    def by_halves(own):
        low = own[:, :, :half]
        high = own[:, :, half:]
        x_high = exchanged(high, "ctx", 1)
        x_low = exchanged(low, "ctx", 1)
        y_low = exchanged(low, "ctx", 2)
        y_high = exchanged(high, "ctx", 2)
        far_high = exchanged(x_high, "ctx", 2)
        far_low = exchanged(y_low, "ctx", 1)
        return [own, x_low, x_high, y_low, y_high, far_low, far_high], HALVES

    def direct(own):
        return [own] + [exchanged(own, "ctx", mask) for mask in (1, 2, 3)], WHOLES

    def two_phases(mine, first_x, first_y, rest_x, rest_y, tail=None):
        got_x = exchanged(first_x, "ctx", 1)
        got_y = exchanged(first_y, "ctx", 2)
        second_x = (rest_x + got_y[:, :, :half].astype(FLOAT)).astype(SHORT)
        second_y = (rest_y + got_x[:, :, :half].astype(FLOAT)).astype(SHORT)
        more_x = exchanged(second_x, "ctx", 1)
        more_y = exchanged(second_y, "ctx", 2)
        if tail is not None:
            more_x, tail = lax.optimization_barrier((more_x, tail))
        low = mine[:, :, :half] + got_x[:, :, half:].astype(FLOAT) + more_y.astype(FLOAT)
        high = mine[:, :, half:] + got_y[:, :, half:].astype(FLOAT) + more_x.astype(FLOAT)
        total = jnp.concatenate([low, high], axis=2).astype(SHORT)
        return total if tail is None else (total, tail)

    gathers = [by_halves, direct]
    pieces = []
    for at, chunk in enumerate(CHUNKS):
        after = []
        if at == 1:
            after = [pieces[0][0][i] for i in (2,)]
        pieces.append(gathers[at](block_of(chunk, after)))
    repeat = queries.shape[3] // keyvals.shape[4]

    def columns(array, start, stop):
        return array[..., start * repeat * DH : stop * repeat * DH]

    key_parts = []
    down_parts = []
    for (start, stop), (own_pieces, parts_of), how in zip(CHUNKS, pieces, [(TWO_PHASES, (FLOAT, SHORT, SHORT, FLOAT, FLOAT), two_phases), (TWO_PHASES, (FLOAT, SHORT, SHORT, FLOAT, FLOAT), two_phases)]):
        targets, types, join = how
        asked, saved = queries[0], saved_out[0]
        gate = gradient if start else own_pieces[3]
        asked, saved = columns(asked, start, stop), columns(saved, start, stop)
        asked, saved, _ = lax.optimization_barrier((asked, saved, gate))
        gradient, *parts = square_layers(
            start, stop - start, meta, asked, columns(grad_in[0], start, stop), saved, own_pieces, parts_of, targets, types
        )
        down_parts.append(shifted(gradient, "section", -1))
        if stop == CHUNKS[-1][1]:
            grad_down = jnp.concatenate(down_parts, axis=1)[None]
            result, grad_down = join(*parts, tail=grad_down)
        else:
            result = join(*parts)
        key_parts.append(result)
    grad_kv = jnp.concatenate(key_parts, axis=3)[None]
    return (grad_kv, grad_down)


def solution(mesh):
    in_specs = (
        P("section", None, "ctx", None),
        P("section", None, None, "ctx", None),
        P("section", None, "ctx", None),
        P("section", "ctx", None),
        P(),
        P(),
    )
    out_specs = (P("section", None, None, "ctx", None), P("section", "ctx", None))
    return jax.shard_map(
        on_device, mesh=mesh, in_specs=in_specs, out_specs=out_specs, check_vma=False
    )
```
